32 devices in a mesh: fsdp: 4 (over y, x), ctx: 4 (over z), tp: 2 (over core).
Axes of the slice: x: 2, y: 2, z: 4, core: 2. Of those that a mesh axis runs over, the one named last changes fastest.
Arguments:
- tokens: bfloat16 [16384, 1024], P(('fsdp', 'ctx')), may hold values from -6 to 6
- lengths: int32 [4, 3], P('fsdp'), may hold values from 1 to 2048, 4096 in all within a row
- cotangent: bfloat16 [16384, 1024], P(('fsdp', 'ctx')), may hold values from -6 to 6
- first_gain: bfloat16 [1024], P('fsdp'), may hold values from 0.099609375 to 1.8984375
- first_bias: bfloat16 [1024], P('fsdp'), may hold values from -1.75 to 1.75
- second_gain: bfloat16 [1024], P('fsdp'), may hold values from 0.099609375 to 1.8984375
- second_bias: bfloat16 [1024], P('fsdp'), may hold values from -1.75 to 1.75
- w_qkv: bfloat16 [3, 1024, 1024], P(None, 'fsdp', 'tp'), may hold values from -0.1875 to 0.1875
- b_qkv: bfloat16 [3, 1024], P(None, 'tp'), may hold values from -1.75 to 1.75
- w_out: bfloat16 [1024, 1024], P('tp', 'fsdp'), may hold values from -3 to 3
- b_out: bfloat16 [1024], P('fsdp'), may hold values from -1.75 to 1.75
- w_up: bfloat16 [1024, 4096], P('fsdp', 'tp'), may hold values from -0.1875 to 0.1875
- b_up: bfloat16 [4096], P('tp'), may hold values from -3 to 3
- w_down: bfloat16 [4096, 1024], P('tp', 'fsdp'), may hold values from -0.09375 to 0.09375
- b_down: bfloat16 [1024], P('fsdp'), may hold values from -1.75 to 1.75
Outputs:
- block_output: bfloat16 [16384, 1024], P(('fsdp', 'ctx'))
- grad_tokens: float32 [16384, 1024], P(('fsdp', 'ctx'))
- grad_first_gain: float32 [1024], P('fsdp')
- grad_first_bias: float32 [1024], P('fsdp')
- grad_second_gain: float32 [1024], P('fsdp')
- grad_second_bias: float32 [1024], P('fsdp')
- grad_w_qkv: float32 [3, 1024, 1024], P(None, 'fsdp', 'tp')
- grad_b_qkv: float32 [3, 1024], P(None, 'tp')
- grad_w_out: float32 [1024, 1024], P('tp', 'fsdp')
- grad_b_out: float32 [1024], P('fsdp')
- grad_w_up: float32 [1024, 4096], P('fsdp', 'tp')
- grad_b_up: float32 [4096], P('tp')
- grad_w_down: float32 [4096, 1024], P('tp', 'fsdp')
- grad_b_down: float32 [1024], P('fsdp')
The draws below stay inside these ranges and needn't reach their ends.
Inputs may be any that keep to these rules, and one draw needn't show every extreme that they name: Each row of lengths sums to 4096 and its longest sequence has exactly 2048 tokens.
All inputs are finite; a program needn't handle non-finite values.
Results may differ from the reference program's by a relative error of at most 0.017.
Values may be sent and summed in bfloat16 or wider, within the bound.
A program may use at most 128 MiB of HBM per device.

```python
import math
import jax
import jax.numpy as jnp
import numpy as np
from jax import lax

D = 1024
H = 16
HD = 64
ROT = 16
FF = 4096
SEQS = 3
ROW = 4096
TOKENS = 16384
N_FSDP = 4


def strengthened(entries, rng, source, target, blocks, factor):
    owner, partner = [(jnp.arange(entries.shape[axis_at]) // (entries.shape[axis_at] // blocks)).reshape([-1 if axis == axis_at else 1 for axis in range(entries.ndim)]) for axis_at in (source, target)]
    chosen = jax.random.permutation(rng, blocks)[partner]
    strong = (owner == chosen) | (owner == (partner + blocks // 2) % blocks)
    return jnp.where(strong, factor * entries, entries)


def block_levels(stream_key, dims, split, least, high):
    level, own = 1.0, jax.random.fold_in(stream_key, 6)
    for dim, shards_of in split:
        draws = jnp.exp(jax.random.uniform(jax.random.fold_in(own, dim), (shards_of,), jnp.float32, least / len(split), high / len(split)))
        level = level * jnp.repeat(draws, dims[dim] // shards_of).reshape([-1 if axis == dim else 1 for axis in range(len(dims))])
    return level


def profile(number_of, total, reach, skew):
    loads = [(1 << 20) // math.isqrt(rank ** skew) + 1 for rank in range(2, number_of + 1)]
    spare, counts = total - reach - (number_of - 1), [1] * (number_of - 1)
    while spare > 0:
        free = [i for i in range(number_of - 1) if counts[i] < reach]
        whole, left = sum([loads[i] for i in free]), spare
        for i in free:
            extra = min(reach - counts[i], max(1, left * loads[i] // whole), spare)
            counts[i] = counts[i] + extra
            spare = spare - extra
    return np.array([reach] + counts)


def ragged(rng, number_of, total, most, skew):
    if number_of == 2:
        one = jax.random.randint(rng, (), max(1, total - most), min(most, total - 1) + 1)
        return jnp.stack([one, total - one])
    sizes = jnp.asarray(profile(number_of, total, most, skew), jnp.int32)
    pairs = (number_of - 1) // 2
    donor, receiver = sizes[1:1 + 2 * pairs:2], sizes[2:2 + 2 * pairs:2]
    room = jnp.minimum(donor - 1, most - receiver)
    shifted = jax.random.randint(jax.random.fold_in(rng, 1), (pairs,), 0, 1 << 20) % (room + 1)
    sizes = sizes.at[1:1 + 2 * pairs:2].set(donor - shifted).at[2:2 + 2 * pairs:2].set(receiver + shifted)
    return sizes[jax.random.permutation(jax.random.fold_in(rng, 2), number_of)]


def scatter_about(stream_key, extent, deviation, limit, cuts=(), kind=jnp.bfloat16):
    drawn = jax.random.normal(stream_key, extent, jnp.float32) * deviation
    if len(cuts) > 0:
        drawn = block_levels(stream_key, extent, cuts, -0.22, 0.18) * drawn
    return jnp.clip(drawn, min=-limit, max=limit).astype(kind)


def heavy_noise(own_key, shape, deviation, most, pieces, heavy, kind=jnp.bfloat16):
    values = deviation * jax.random.normal(own_key, shape, jnp.float32)
    if pieces:
        values = values * block_levels(own_key, shape, pieces, -0.22, 0.18)
    return jnp.clip(strengthened(values, jax.random.fold_in(own_key, 3), *heavy), -most, most).astype(kind)


def setup_inputs(seed: int = 0) -> dict:
    key_list = jax.random.split(jax.random.key(seed), 16)
    return {
        "tokens": scatter_about(key_list[0], (TOKENS, D), 1.0, 6.0, ((0, 16),)),
        "lengths": jax.vmap(lambda own: ragged(own, SEQS, ROW, ROW // 2, 2))(jax.random.split(key_list[1], N_FSDP)).reshape((N_FSDP, SEQS)).astype(jnp.int32),
        "cotangent": heavy_noise(key_list[2], (TOKENS, D), 1.0, 6.0, ((0, 16),), (0, 1, 16, 2.0)),
        "first_gain": jnp.clip(1.0 + 0.18 * jax.random.normal(key_list[3], (D,), jnp.float32), 0.099609375, 1.8984375).astype(jnp.bfloat16),
        "first_bias": scatter_about(key_list[4], (D,), 0.3, 1.75, ((0, 4),)),
        "second_gain": jnp.clip(1.0 + 0.18 * jax.random.normal(key_list[5], (D,), jnp.float32), 0.099609375, 1.8984375).astype(jnp.bfloat16),
        "second_bias": scatter_about(key_list[6], (D,), 0.3, 1.75, ((0, 4),)),
        "w_qkv": scatter_about(key_list[7], (3, D, D), D ** -0.5, 0.1875, ((1, 4), (2, 2))),
        "b_qkv": scatter_about(key_list[8], (3, D), 0.3, 1.75, ((1, 2),)),
        "w_out": scatter_about(key_list[9], (D, D), 0.5, 3.0, ((0, 2), (1, 4))),
        "b_out": scatter_about(key_list[10], (D,), 0.3, 1.75, ((0, 4),)),
        "w_up": scatter_about(key_list[11], (D, FF), D ** -0.5, 0.1875, ((0, 4), (1, 2))),
        "b_up": scatter_about(key_list[12], (FF,), 0.5, 3.0, ((0, 2),)),
        "w_down": scatter_about(key_list[13], (FF, D), FF ** -0.5, 0.09375, ((0, 2), (1, 4))),
        "b_down": scatter_about(key_list[14], (D,), 0.3, 1.75, ((0, 4),)),
    }


@jax.custom_vjp
def low(v):
    return lax.optimization_barrier(v.astype(jnp.bfloat16)).astype(jnp.float32)

@jax.custom_vjp
def low_back(v):
    return v

def low_keep(v):
    return (low(v), None)

def low_pass(kept, grad):
    return (grad,)

def back_keep(v):
    return (v, None)

def back_low(kept, grad):
    return (low(grad),)
low.defvjp(low_keep, low_pass)
low_back.defvjp(back_keep, back_low)

def layer_norm(values, gain, shift):
    centre = values - lax.optimization_barrier(jnp.mean(values, axis=-1, keepdims=True))
    spread = lax.optimization_barrier(jnp.mean(centre * centre, axis=-1, keepdims=True))
    return centre * lax.rsqrt(spread + 1e-05) * gain + shift

def rotary_tables(position, rotary):
    halves = rotary // 2
    base_rates = jnp.power(10000.0, -2.0 * jnp.arange(halves, dtype=jnp.float32) / rotary)
    angles = position.astype(jnp.float32)[:, None] * base_rates[None, :]
    return (jnp.cos(angles), jnp.sin(angles))

def rotate(values, cosine, sine_table, rotary):
    halves = rotary // 2
    former = values[..., :halves]
    latter = values[..., halves:rotary]
    cos_wide = cosine[:, None, :]
    sin_wide = sine_table[:, None, :]
    return jnp.concatenate([former * cos_wide - latter * sin_wide, latter * cos_wide + former * sin_wide, values[..., rotary:]], axis=-1)

def segment_info(seq_lengths, offset, place_count):
    seq_ends = jnp.cumsum(seq_lengths).astype(jnp.int32)
    starts = (seq_ends - seq_lengths).astype(jnp.int32)
    places = (offset + jnp.arange(place_count, dtype=jnp.int32)).astype(jnp.int32)
    inside = (places[:, None] >= starts[None, :]) & (places[:, None] < seq_ends[None, :])
    labels = jnp.arange(seq_lengths.shape[0], dtype=jnp.int32)
    segment = lax.optimization_barrier(jnp.sum(jnp.where(inside, labels[None, :], 0), axis=1)).astype(jnp.int32)
    position = (places - lax.optimization_barrier(jnp.sum(jnp.where(inside, starts[None, :], 0), axis=1))).astype(jnp.int32)
    return (places, segment, position)

def attend_block(block_index, query_rows, key_rows, value_rows, places, segment):
    block_rows = min(512, query_rows.shape[0])
    first_row = (block_index * block_rows).astype(jnp.int32)
    query_block = lax.dynamic_slice_in_dim(query_rows, first_row, block_rows, 0)
    query_place = lax.dynamic_slice_in_dim(places, first_row, block_rows, 0)
    query_segment = lax.dynamic_slice_in_dim(segment, first_row, block_rows, 0)
    scores = jnp.einsum('qhd,khd->hqk', query_block, key_rows, precision=lax.Precision.HIGHEST) * HD ** (-0.5)
    scores = low_back(scores)
    visible = (segment[None, :] == query_segment[:, None]) & (places[None, :] <= query_place[:, None])
    scores = jnp.where(visible[None], scores, -1e+30)
    largest = lax.optimization_barrier(jnp.max(scores, axis=-1, keepdims=True))
    exp_terms = jnp.exp(scores - largest)
    weights_full = exp_terms / lax.optimization_barrier(jnp.sum(exp_terms, axis=-1, keepdims=True))
    return jnp.einsum('hqk,khd->qhd', low(weights_full), value_rows, precision=lax.Precision.HIGHEST)

def attend_row(query_rows, key_rows, value_rows, places, segment):
    block_rows = min(512, query_rows.shape[0])
    block_count = query_rows.shape[0] // block_rows
    checked = jax.checkpoint(attend_block)
    mixed = lax.map(lambda block_index: checked(block_index, query_rows, key_rows, value_rows, places, segment), jnp.arange(block_count, dtype=jnp.int32))
    return mixed.reshape(query_rows.shape[0], -1)

def row_forward(token_row, seq_lengths, weights):
    first_gain, first_bias, second_gain, second_bias, w_qkv, b_qkv, w_out, b_out, w_up, b_up, w_down, b_down = weights
    places, segment, position = segment_info(seq_lengths, 0, ROW)
    cosine, sine_table = rotary_tables(position, ROT)
    normed_one = low(layer_norm(token_row, first_gain, first_bias))
    linear = jnp.einsum('td,ide->ite', normed_one, w_qkv, precision=lax.Precision.HIGHEST) + b_qkv[:, None, :]
    linear = low_back(linear)
    query_rows = low(rotate(linear[0].reshape(ROW, H, HD), cosine, sine_table, ROT))
    key_rows = low(rotate(linear[1].reshape(ROW, H, HD), cosine, sine_table, ROT))
    value_rows = low(linear[2].reshape(ROW, H, HD))
    attention = low_back(low(attend_row(query_rows, key_rows, value_rows, places, segment)))
    normed_two = low(layer_norm(token_row, second_gain, second_bias))
    hidden_pre = low_back(jnp.dot(normed_two, w_up, precision=lax.Precision.HIGHEST) + b_up)
    hidden = low(jax.nn.gelu(hidden_pre, approximate=False))
    attn_branch = jnp.dot(attention, w_out, precision=lax.Precision.HIGHEST) + b_out
    ffn_branch = jnp.dot(hidden, w_down, precision=lax.Precision.HIGHEST) + b_down
    return token_row + attn_branch + ffn_branch

def reference(tokens, lengths, cotangent, first_gain, first_bias, second_gain, second_bias, w_qkv, b_qkv, w_out, b_out, w_up, b_up, w_down, b_down):
    params = tuple((member.astype(jnp.float32) for member in (first_gain, first_bias, second_gain, second_bias, w_qkv, b_qkv, w_out, b_out, w_up, b_up, w_down, b_down)))
    token_rows = tokens.astype(jnp.float32).reshape(N_FSDP, ROW, D)
    cot_rows = cotangent.astype(jnp.float32).reshape(N_FSDP, ROW, D)
    checked_row = jax.checkpoint(row_forward)

    def whole_block(rows_in, weights):

        def advance(carry_sum, pair_item):
            return (carry_sum, checked_row(pair_item[0], pair_item[1], weights))
        unused, outputs = lax.scan(advance, jnp.zeros((), jnp.float32), (rows_in, lengths))
        return outputs
    outputs, pullback = jax.vjp(whole_block, token_rows, params)
    grad_rows, grads = pullback(cot_rows)
    return (outputs.reshape(N_FSDP * ROW, D).astype(jnp.bfloat16), grad_rows.reshape(N_FSDP * ROW, D), grads[0], grads[1], grads[2], grads[3], grads[4], grads[5], grads[6], grads[7], grads[8], grads[9], grads[10], grads[11])
```

```python
import functools

import jax
import jax.numpy as jnp
from jax import lax
from jax.experimental import pallas as pl
from jax.experimental.pallas import tpu as pltpu
from jax.sharding import PartitionSpec as P

HD = 64
ROT = 16
BQ = 512
BK = 512
PAIR = 2 * HD
F32 = jnp.float32
BF16 = jnp.bfloat16
LOWEST = -1e30
NT = (((1,), (1,)), ((), ()))
TN = (((0,), (0,)), ((), ()))


def dot(a, b, dims=(((1,), (0,)), ((), ()))):
    return lax.dot_general(a, b, dims, preferred_element_type=F32)


def head_masks(rows):
    lane = lax.broadcasted_iota(jnp.int32, (rows, PAIR), 1)
    return (lane < HD, lane >= HD)


def key_loops(body, low_ref, full_ref, q_index, base, key_rows, state):
    last = jnp.minimum((base_blocks(base) + (q_index + 1) * BQ) // BK, key_rows // BK)
    diagonal = jnp.minimum((base_blocks(base) + q_index * BQ) // BK, key_rows // BK)
    low = jnp.minimum(low_ref[q_index], last)
    full = jnp.clip(full_ref[q_index], low, jnp.maximum(diagonal, low))
    diagonal = jnp.maximum(diagonal, full)
    state = lax.fori_loop(low, full, functools.partial(body, True), state)
    state = lax.fori_loop(full, diagonal, functools.partial(body, False), state)
    return lax.fori_loop(diagonal, last, functools.partial(body, True), state)


def base_blocks(base):
    return base


def seen(key_block, start_row, place_row):
    at = key_block * BK + lax.broadcasted_iota(jnp.int32, (BK, BQ), 0)
    return (at >= start_row) & (at <= place_row)


def forward_kernel(base, low_ref, full_ref, q_ref, k_ref, v_ref, g_ref, start_ref, place_ref, out_ref, lse_ref, delta_ref, vt_ref):
    q_index = pl.program_id(1)
    key_rows = k_ref.shape[0]

    @pl.when(q_index == 0)
    def _():
        vt_ref[...] = v_ref[...].T

    masks = head_masks(BQ)
    q = q_ref[...]
    heads = [jnp.where(mask, q, jnp.zeros_like(q)) for mask in masks]
    start_row, place_row = start_ref[0:1, :], place_ref[0:1, :]

    def body(masked, block, state):
        first = pl.multiple_of(block * BK, BK)
        k = k_ref[pl.ds(first, BK), :]
        after = []
        for i in range(2):
            top, total, mixed = state[i]
            scores = dot(k, heads[i], NT)
            if masked:
                scores = jnp.where(seen(block, start_row, place_row), scores, LOWEST)
            new_top = jnp.maximum(top, jnp.max(scores, axis=0, keepdims=True))
            shrink = jnp.exp(top - new_top)
            terms = jnp.exp(scores - new_top)
            total = total * shrink + jnp.sum(terms, axis=0, keepdims=True)
            vt = vt_ref[i * HD : (i + 1) * HD, pl.ds(first, BK)]
            mixed = mixed * shrink + dot(vt, terms.astype(BF16))
            after.append((new_top, total, mixed))
        return tuple(after)

    fresh = (jnp.full((1, BQ), LOWEST, F32), jnp.zeros((1, BQ), F32), jnp.zeros((HD, BQ), F32))
    state = key_loops(body, low_ref, full_ref, q_index, base, key_rows, (fresh, fresh))
    mixes = [mixed / total for _, total, mixed in state]
    mix = jnp.concatenate(mixes, axis=0)
    out_ref[...] = mix.T.astype(BF16)
    weighted = mix * g_ref[...].astype(F32).T
    lse_ref[0] = jnp.concatenate([top + jnp.log(total) for top, total, _ in state], axis=0)
    delta_ref[0] = jnp.concatenate(
        [jnp.sum(weighted[i * HD : (i + 1) * HD], axis=0, keepdims=True) for i in range(2)], axis=0
    )


def backward_kernel(base, low_ref, full_ref, q_ref, k_ref, v_ref, g_ref, start_ref, place_ref, lse_ref, delta_ref, dq_ref, dk_ref, dv_ref, kt_ref, dk_sum, dv_sum):
    q_index = pl.program_id(1)
    key_rows = k_ref.shape[0]

    @pl.when(q_index == 0)
    def _():
        kt_ref[...] = k_ref[...].T
        dk_sum[...] = jnp.zeros_like(dk_sum)
        dv_sum[...] = jnp.zeros_like(dv_sum)

    masks = head_masks(BQ)
    q, g = q_ref[...], g_ref[...]
    heads = [jnp.where(mask, q, jnp.zeros_like(q)) for mask in masks]
    grads = [jnp.where(mask, g, jnp.zeros_like(g)) for mask in masks]
    start_row, place_row = start_ref[0:1, :], place_ref[0:1, :]

    def body(masked, block, state):
        first = pl.multiple_of(block * BK, BK)
        k = k_ref[pl.ds(first, BK), :]
        v = v_ref[pl.ds(first, BK), :]
        after, dks, dvs = [], [], []
        for i in range(2):
            scores = dot(k, heads[i], NT)
            if masked:
                scores = jnp.where(seen(block, start_row, place_row), scores, LOWEST)
            prob = jnp.exp(scores - lse_ref[0, i : i + 1, :])
            dprob = dot(v, grads[i], NT)
            dscores = (prob * (dprob - delta_ref[0, i : i + 1, :])).astype(BF16)
            dvs.append(dot(prob.astype(BF16), grads[i]))
            dks.append(dot(dscores, heads[i]))
            kt = kt_ref[i * HD : (i + 1) * HD, pl.ds(first, BK)]
            after.append(state[i] + dot(kt, dscores))
        dk_sum[pl.ds(first, BK), :] += dks[0] + dks[1]
        dv_sum[pl.ds(first, BK), :] += dvs[0] + dvs[1]
        return tuple(after)

    fresh = jnp.zeros((HD, BQ), F32)
    state = key_loops(body, low_ref, full_ref, q_index, base, key_rows, (fresh, fresh))
    dq_ref[...] = jnp.concatenate(state, axis=0).T * (HD**-0.5)

    @pl.when(q_index == pl.num_programs(1) - 1)
    def _():
        dk_ref[...] = dk_sum[...].astype(dk_ref.dtype)
        dv_ref[...] = dv_sum[...].astype(dv_ref.dtype)


def attention_call(kernel, base, bounds, q, k, v, g, rows, extra, kind):
    tokens, width = q.shape
    keys = k.shape[0]
    pairs = width // PAIR
    by_query = pl.BlockSpec((BQ, PAIR), lambda p, i, *_: (i, p))
    by_key = pl.BlockSpec((keys, PAIR), lambda p, i, *_: (0, p))
    by_row = pl.BlockSpec((8, BQ), lambda p, i, *_: (0, i))
    by_stat = pl.BlockSpec((1, 2, BQ), lambda p, i, *_: (p, 0, i))
    stat = jax.ShapeDtypeStruct((pairs, 2, tokens), F32)
    in_specs = [by_query, by_key, by_key, by_query, by_row, by_row]
    scratch = [pltpu.VMEM((PAIR, keys), BF16)]
    area = tokens * keys * width
    if kind == "forward":
        out_shape = [jax.ShapeDtypeStruct((tokens, width), BF16), stat, stat]
        out_specs = [by_query, by_stat, by_stat]
        flops = 4 * area
    else:
        in_specs += [by_stat, by_stat]
        key_kind = jax.ShapeDtypeStruct((keys, width), kind)
        out_shape = [jax.ShapeDtypeStruct((tokens, width), F32), key_kind, key_kind]
        out_specs = [by_query, by_key, by_key]
        scratch += [pltpu.VMEM((keys, PAIR), F32)] * 2
        flops = 10 * area
    return pl.pallas_call(
        functools.partial(kernel, base),
        grid_spec=pltpu.PrefetchScalarGridSpec(
            num_scalar_prefetch=2,
            grid=(pairs, tokens // BQ),
            in_specs=in_specs,
            out_specs=out_specs,
            scratch_shapes=scratch,
        ),
        out_shape=out_shape,
        cost_estimate=pl.CostEstimate(
            flops=flops, bytes_accessed=8 * keys * width, transcendentals=area // HD
        ),
    )(*bounds, q, k, v, g, *rows, *extra)


def turn_kernel(tables, turned, scales, *refs):
    cos_ref, sin_ref = refs[0], refs[1]
    count = len(turned)
    lane = lax.broadcasted_iota(jnp.int32, cos_ref.shape, 1) % HD
    for index in range(count):
        src, out = refs[2 + index], refs[2 + 2 * count + index]
        bias = refs[2 + count + index]
        for p in range(src.shape[1] // PAIR):
            cut = slice(p * PAIR, (p + 1) * PAIR)
            x = src[:, cut].astype(F32) + bias[0:1, cut]
            if turned[index]:
                partner = jnp.where(
                    lane < ROT // 2, pltpu.roll(x, PAIR - ROT // 2, 1), pltpu.roll(x, ROT // 2, 1)
                )
                x = x * cos_ref[...] + partner * sin_ref[...]
            out[:, cut] = (x * scales[index]).astype(BF16)


def turn(tables, sources, biases, turned, scales):
    rows, width = sources[0].shape
    step = 256
    table = pl.BlockSpec((step, PAIR), lambda i: (i, 0))
    block = pl.BlockSpec((step, width), lambda i: (i, 0))
    single = pl.BlockSpec((8, width), lambda i: (0, 0))
    count = len(sources)
    return pl.pallas_call(
        functools.partial(turn_kernel, None, turned, scales),
        grid=(rows // step,),
        in_specs=[table, table] + [block] * count + [single] * count,
        out_specs=[block] * count,
        out_shape=[jax.ShapeDtypeStruct((rows, width), BF16)] * count,
        cost_estimate=pl.CostEstimate(
            flops=10 * rows * width * count, bytes_accessed=6 * rows * width * count, transcendentals=0
        ),
    )(*tables, *sources, *biases)


def wide_tables(position):
    lane = jnp.arange(PAIR, dtype=jnp.int32) % HD
    halves = ROT // 2
    rates = jnp.power(10000.0, -2.0 * jnp.arange(halves, dtype=F32) / ROT)[lane % halves]
    angles = position.astype(F32)[:, None] * rates[None, :]
    cosine = jnp.where(lane < ROT, jnp.cos(angles), 1.0)
    sine = jnp.sin(angles)
    signed = jnp.where(lane < halves, -sine, jnp.where(lane < ROT, sine, 0.0))
    return cosine, signed


def settle(value):
    return lax.optimization_barrier(value.astype(BF16))


def pair_sum(value):
    own = settle(value)
    other = lax.ppermute(own, "tp", [(0, 1), (1, 0)])
    return own.astype(F32) + other.astype(F32)


def on_device(
    tokens,
    lengths,
    cotangent,
    first_gain,
    first_bias,
    second_gain,
    second_bias,
    w_qkv,
    b_qkv,
    w_out,
    b_out,
    w_up,
    b_up,
    w_down,
    b_down,
):
    token_rows, model = tokens.shape
    ctx = lax.axis_size("ctx")
    row_total = token_rows * ctx
    rank = lax.axis_index("ctx")
    place_first = rank * token_rows
    longest = row_total // 2
    behind = min(-(-(longest - 1) // token_rows), ctx - 1)
    small = jnp.stack([first_gain, first_bias, second_gain, second_bias, b_out, b_down])
    small = lax.all_gather(small, "fsdp", axis=1, tiled=True).astype(F32)
    gain_one, bias_one, gain_two, bias_two, out_bias, down_bias = [small[i] for i in range(6)]
    qkv_full = lax.all_gather(w_qkv, "fsdp", axis=1, tiled=True)
    up_full = lax.all_gather(w_up, "fsdp", axis=0, tiled=True)
    down_full = lax.all_gather(w_down, "fsdp", axis=1, tiled=True)
    out_full = lax.all_gather(w_out, "fsdp", axis=1, tiled=True)

    seq_ends = jnp.cumsum(lengths[0])
    starts = seq_ends - lengths[0]
    places = place_first + jnp.arange(token_rows, dtype=jnp.int32)
    inside = (places[:, None] >= starts[None, :]) & (places[:, None] < seq_ends[None, :])
    start = jnp.sum(jnp.where(inside, starts[None, :], 0), axis=1).astype(jnp.int32)
    tables = wide_tables(places - start)
    shift = place_first - behind * token_rows
    start_ext = start - shift
    place_ext = places - shift
    rows = [jnp.broadcast_to(r[None, :], (8, token_rows)) for r in (start_ext, place_ext)]
    low = start_ext[::BQ] // BK
    full = -(-start_ext[BQ - 1 :: BQ] // BK)
    base = behind * token_rows
    near = [r - base for r in rows]
    near_bounds = (jnp.maximum(low - base // BK, 0), jnp.maximum(full - base // BK, 0))

    x = tokens.astype(F32)
    centre = x - jnp.mean(x, axis=-1, keepdims=True)
    scale = lax.rsqrt(jnp.mean(centre * centre, axis=-1, keepdims=True) + 1e-05)
    normal = centre * scale
    normed_one = (normal * gain_one + bias_one).astype(BF16)
    normed_two = (normal * gain_two + bias_two).astype(BF16)

    linear = [dot(normed_one, qkv_full[i]) for i in range(3)]
    lifted = [jnp.broadcast_to(b_qkv[i].astype(F32)[None, :], (8, b_qkv.shape[1])) for i in range(3)]
    queries, keys, values = turn(
        tables, linear, lifted, (True, True, False), (HD**-0.5, 1.0, 1.0)
    )
    far_keys, far_values = [], []
    for back in range(behind, 0, -1):
        ahead = [(s, s + back) for s in range(ctx - back)]
        far_keys.append(lax.ppermute(keys, "ctx", ahead))
        far_values.append(lax.ppermute(values, "ctx", ahead))
    keys_far, values_far = jnp.concatenate(far_keys), jnp.concatenate(far_values)
    keys_all, values_all = jnp.concatenate([keys_far, keys]), jnp.concatenate([values_far, values])

    hidden_pre = dot(normed_two, up_full) + b_up.astype(F32)
    hidden, gelu_pull = jax.vjp(lambda v: jax.nn.gelu(v, approximate=False), hidden_pre)
    hidden = hidden.astype(BF16)
    grad_hidden = dot(cotangent, down_full, NT)
    grad_hidden_pre = gelu_pull(grad_hidden)[0].astype(BF16)
    grad_attention = dot(cotangent, out_full, NT).astype(BF16)
    grad_w_down = dot(hidden, cotangent, TN)
    grad_w_up = dot(normed_two, grad_hidden_pre, TN)
    grad_b_up = jnp.sum(grad_hidden_pre.astype(F32), axis=0)
    error_two = dot(grad_hidden_pre, up_full, NT)

    def reduced(grad, dim):
        part = lax.psum_scatter(grad.astype(BF16), "fsdp", scatter_dimension=dim, tiled=True)
        return lax.psum(part, "ctx").astype(F32)

    part_down = reduced(grad_w_down, 1)
    part_up = reduced(grad_w_up, 0)

    attention, lse, delta = attention_call(
        forward_kernel, base, (low, full), queries, keys_all, values_all, grad_attention, rows, (), "forward"
    )
    dq_far, dk_far, dv_far = attention_call(
        backward_kernel, base, (low, full), queries, keys_far, values_far, grad_attention, rows, (lse, delta), BF16
    )
    arrived_keys, arrived_values = [], []
    for index, back in enumerate(range(behind, 0, -1)):
        returning = [(s + back, s) for s in range(ctx - back)]
        cut = slice(index * token_rows, (index + 1) * token_rows)
        arrived_keys.append(lax.ppermute(dk_far[cut], "ctx", returning))
        arrived_values.append(lax.ppermute(dv_far[cut], "ctx", returning))
    dq_near, dk_near, dv_near = attention_call(
        backward_kernel, 0, near_bounds, queries, keys, values, grad_attention, near, (lse, delta), F32
    )
    branches = pair_sum(dot(attention, out_full) + dot(hidden, down_full))
    block_output = (x + branches + out_bias + down_bias).astype(BF16)
    part_out = reduced(dot(attention, cotangent, TN), 1)

    zero = jnp.zeros((8, queries.shape[1]), F32)
    undo = (tables[0], -tables[1])
    (grad_linear_q,) = turn(undo, [dq_far + dq_near], [zero], (True,), (1.0,))
    grad_k = functools.reduce(lambda a, b: a + b.astype(F32), arrived_keys, dk_near)
    grad_v = functools.reduce(lambda a, b: a + b.astype(F32), arrived_values, dv_near)
    grad_linear_k, grad_linear_v = turn(undo, [grad_k, grad_v], [zero, zero], (True, False), (1.0, 1.0))
    grad_linear = [grad_linear_q, grad_linear_k, grad_linear_v]
    part_qkv = jnp.stack([reduced(dot(normed_one, part, TN), 0) for part in grad_linear])
    grad_b_qkv = [jnp.sum(part.astype(F32), axis=0) for part in grad_linear]
    error_one = sum(dot(part, qkv_full[i], NT) for i, part in enumerate(grad_linear))

    whole = pair_sum(error_one * gain_one + error_two * gain_two)
    grad_tokens = cotangent.astype(F32) + scale * (
        whole
        - jnp.mean(whole, axis=-1, keepdims=True)
        - normal * jnp.mean(whole * normal, axis=-1, keepdims=True)
    )
    shared = jnp.concatenate(
        [
            jnp.sum(error_one * normal, axis=0),
            jnp.sum(error_one, axis=0),
            jnp.sum(error_two * normal, axis=0),
            jnp.sum(error_two, axis=0),
        ]
    )
    shared = shared + lax.ppermute(shared, "tp", [(0, 1), (1, 0)])
    grad_bias = jnp.sum(cotangent.astype(F32), axis=0)
    vector = lax.psum(jnp.concatenate([shared, grad_bias, *grad_b_qkv, grad_b_up]), ("fsdp", "ctx"))
    width = b_qkv.shape[1]
    owned = first_gain.shape[0]
    mine = lax.dynamic_slice_in_dim(
        vector[: 5 * model].reshape(5, model), lax.axis_index("fsdp") * owned, owned, 1
    )
    rest = vector[5 * model :]
    return (
        block_output,
        grad_tokens,
        mine[0],
        mine[1],
        mine[2],
        mine[3],
        part_qkv,
        rest[: 3 * width].reshape(3, width),
        part_out,
        mine[4],
        part_up,
        rest[3 * width :],
        part_down,
        mine[4],
    )


def solution(mesh):
    placed = (
        P(("fsdp", "ctx"), None),
        P("fsdp", None),
        P(("fsdp", "ctx"), None),
        P("fsdp"),
        P("fsdp"),
        P("fsdp"),
        P("fsdp"),
        P(None, "fsdp", "tp"),
        P(None, "tp"),
        P("tp", "fsdp"),
        P("fsdp"),
        P("fsdp", "tp"),
        P("tp"),
        P("tp", "fsdp"),
        P("fsdp"),
    )
    return jax.shard_map(
        on_device,
        mesh=mesh,
        in_specs=placed,
        out_specs=(
            P(("fsdp", "ctx"), None),
            P(("fsdp", "ctx"), None),
            P("fsdp"),
            P("fsdp"),
            P("fsdp"),
            P("fsdp"),
            P(None, "fsdp", "tp"),
            P(None, "tp"),
            P("tp", "fsdp"),
            P("fsdp"),
            P("fsdp", "tp"),
            P("tp"),
            P("tp", "fsdp"),
            P("fsdp"),
        ),
        check_vma=False,
    )
```

```python
import functools

import jax
import jax.numpy as jnp
from jax import lax
from jax.experimental import pallas as pl
from jax.experimental.pallas import tpu as pltpu
from jax.sharding import PartitionSpec as P

HD = 64
ROT = 16
BQ = 512
BK = 512
PAIR = 2 * HD
F32 = jnp.float32
BF16 = jnp.bfloat16
LOWEST = -1e30
NT = (((1,), (1,)), ((), ()))
TN = (((0,), (0,)), ((), ()))


def dot(a, b, dims=(((1,), (0,)), ((), ()))):
    return lax.dot_general(a, b, dims, preferred_element_type=F32)


def head_masks(rows):
    lane = lax.broadcasted_iota(jnp.int32, (rows, PAIR), 1)
    return (lane < HD, lane >= HD)


def key_loops(body, low_ref, full_ref, q_index, base, key_rows, state):
    last = jnp.minimum((base_blocks(base) + (q_index + 1) * BQ) // BK, key_rows // BK)
    diagonal = jnp.minimum((base_blocks(base) + q_index * BQ) // BK, key_rows // BK)
    low = jnp.minimum(low_ref[q_index], last)
    full = jnp.clip(full_ref[q_index], low, jnp.maximum(diagonal, low))
    diagonal = jnp.maximum(diagonal, full)
    state = lax.fori_loop(low, full, functools.partial(body, True), state)
    state = lax.fori_loop(full, diagonal, functools.partial(body, False), state)
    return lax.fori_loop(diagonal, last, functools.partial(body, True), state)


def base_blocks(base):
    return base


def seen(key_block, start_row, place_row):
    at = key_block * BK + lax.broadcasted_iota(jnp.int32, (BK, BQ), 0)
    return (at >= start_row) & (at <= place_row)


def forward_kernel(base, low_ref, full_ref, q_ref, k_ref, v_ref, g_ref, start_ref, place_ref, out_ref, lse_ref, delta_ref, vt_ref):
    q_index = pl.program_id(1)
    key_rows = k_ref.shape[0]

    @pl.when(q_index == 0)
    def _():
        vt_ref[...] = v_ref[...].T

    masks = head_masks(BQ)
    q = q_ref[...]
    heads = [jnp.where(mask, q, jnp.zeros_like(q)) for mask in masks]
    start_row, place_row = start_ref[0:1, :], place_ref[0:1, :]

    def body(masked, block, state):
        first = pl.multiple_of(block * BK, BK)
        k = k_ref[pl.ds(first, BK), :]
        after = []
        for i in range(2):
            top, total, mixed = state[i]
            scores = dot(k, heads[i], NT)
            if masked:
                scores = jnp.where(seen(block, start_row, place_row), scores, LOWEST)
            new_top = jnp.maximum(top, jnp.max(scores, axis=0, keepdims=True))
            shrink = jnp.exp(top - new_top)
            terms = jnp.exp(scores - new_top)
            total = total * shrink + jnp.sum(terms, axis=0, keepdims=True)
            vt = vt_ref[i * HD : (i + 1) * HD, pl.ds(first, BK)]
            mixed = mixed * shrink + dot(vt, terms.astype(BF16))
            after.append((new_top, total, mixed))
        return tuple(after)

    fresh = (jnp.full((1, BQ), LOWEST, F32), jnp.zeros((1, BQ), F32), jnp.zeros((HD, BQ), F32))
    state = key_loops(body, low_ref, full_ref, q_index, base, key_rows, (fresh, fresh))
    mixes = [mixed / total for _, total, mixed in state]
    mix = jnp.concatenate(mixes, axis=0)
    out_ref[...] = mix.T.astype(BF16)
    weighted = mix * g_ref[...].astype(F32).T
    lse_ref[0] = jnp.concatenate([top + jnp.log(total) for top, total, _ in state], axis=0)
    delta_ref[0] = jnp.concatenate(
        [jnp.sum(weighted[i * HD : (i + 1) * HD], axis=0, keepdims=True) for i in range(2)], axis=0
    )


def backward_kernel(base, low_ref, full_ref, q_ref, k_ref, v_ref, g_ref, start_ref, place_ref, lse_ref, delta_ref, dq_ref, dk_ref, dv_ref, kt_ref, dk_sum, dv_sum):
    q_index = pl.program_id(1)
    key_rows = k_ref.shape[0]

    @pl.when(q_index == 0)
    def _():
        kt_ref[...] = k_ref[...].T
        dk_sum[...] = jnp.zeros_like(dk_sum)
        dv_sum[...] = jnp.zeros_like(dv_sum)

    masks = head_masks(BQ)
    q, g = q_ref[...], g_ref[...]
    heads = [jnp.where(mask, q, jnp.zeros_like(q)) for mask in masks]
    grads = [jnp.where(mask, g, jnp.zeros_like(g)) for mask in masks]
    start_row, place_row = start_ref[0:1, :], place_ref[0:1, :]

    def body(masked, block, state):
        first = pl.multiple_of(block * BK, BK)
        k = k_ref[pl.ds(first, BK), :]
        v = v_ref[pl.ds(first, BK), :]
        after, dks, dvs = [], [], []
        for i in range(2):
            scores = dot(k, heads[i], NT)
            if masked:
                scores = jnp.where(seen(block, start_row, place_row), scores, LOWEST)
            prob = jnp.exp(scores - lse_ref[0, i : i + 1, :])
            dprob = dot(v, grads[i], NT)
            dscores = (prob * (dprob - delta_ref[0, i : i + 1, :])).astype(BF16)
            dvs.append(dot(prob.astype(BF16), grads[i]))
            dks.append(dot(dscores, heads[i]))
            kt = kt_ref[i * HD : (i + 1) * HD, pl.ds(first, BK)]
            after.append(state[i] + dot(kt, dscores))
        dk_sum[pl.ds(first, BK), :] += dks[0] + dks[1]
        dv_sum[pl.ds(first, BK), :] += dvs[0] + dvs[1]
        return tuple(after)

    fresh = jnp.zeros((HD, BQ), F32)
    state = key_loops(body, low_ref, full_ref, q_index, base, key_rows, (fresh, fresh))
    dq_ref[...] = jnp.concatenate(state, axis=0).T * (HD**-0.5)

    @pl.when(q_index == pl.num_programs(1) - 1)
    def _():
        dk_ref[...] = dk_sum[...].astype(dk_ref.dtype)
        dv_ref[...] = dv_sum[...].astype(dv_ref.dtype)


def attention_call(kernel, base, bounds, q, k, v, g, rows, extra, kind):
    tokens, width = q.shape
    keys = k.shape[0]
    pairs = width // PAIR
    by_query = pl.BlockSpec((BQ, PAIR), lambda p, i, *_: (i, p))
    by_key = pl.BlockSpec((keys, PAIR), lambda p, i, *_: (0, p))
    by_row = pl.BlockSpec((8, BQ), lambda p, i, *_: (0, i))
    by_stat = pl.BlockSpec((1, 2, BQ), lambda p, i, *_: (p, 0, i))
    stat = jax.ShapeDtypeStruct((pairs, 2, tokens), F32)
    in_specs = [by_query, by_key, by_key, by_query, by_row, by_row]
    scratch = [pltpu.VMEM((PAIR, keys), BF16)]
    area = tokens * keys * width
    if kind == "forward":
        out_shape = [jax.ShapeDtypeStruct((tokens, width), BF16), stat, stat]
        out_specs = [by_query, by_stat, by_stat]
        flops = 4 * area
    else:
        in_specs += [by_stat, by_stat]
        key_kind = jax.ShapeDtypeStruct((keys, width), kind)
        out_shape = [jax.ShapeDtypeStruct((tokens, width), F32), key_kind, key_kind]
        out_specs = [by_query, by_key, by_key]
        scratch += [pltpu.VMEM((keys, PAIR), F32)] * 2
        flops = 10 * area
    return pl.pallas_call(
        functools.partial(kernel, base),
        grid_spec=pltpu.PrefetchScalarGridSpec(
            num_scalar_prefetch=2,
            grid=(pairs, tokens // BQ),
            in_specs=in_specs,
            out_specs=out_specs,
            scratch_shapes=scratch,
        ),
        out_shape=out_shape,
        cost_estimate=pl.CostEstimate(
            flops=flops, bytes_accessed=8 * keys * width, transcendentals=area // HD
        ),
    )(*bounds, q, k, v, g, *rows, *extra)


def turn_kernel(tables, turned, scales, *refs):
    cos_ref, sin_ref = refs[0], refs[1]
    count = len(turned)
    lane = lax.broadcasted_iota(jnp.int32, cos_ref.shape, 1) % HD
    for index in range(count):
        src, out = refs[2 + index], refs[2 + 2 * count + index]
        bias = refs[2 + count + index]
        for p in range(src.shape[1] // PAIR):
            cut = slice(p * PAIR, (p + 1) * PAIR)
            x = src[:, cut].astype(F32) + bias[0:1, cut]
            if turned[index]:
                partner = jnp.where(
                    lane < ROT // 2, pltpu.roll(x, PAIR - ROT // 2, 1), pltpu.roll(x, ROT // 2, 1)
                )
                x = x * cos_ref[...] + partner * sin_ref[...]
            out[:, cut] = (x * scales[index]).astype(BF16)


def turn(tables, sources, biases, turned, scales):
    rows, width = sources[0].shape
    step = 256
    table = pl.BlockSpec((step, PAIR), lambda i: (i, 0))
    block = pl.BlockSpec((step, width), lambda i: (i, 0))
    single = pl.BlockSpec((8, width), lambda i: (0, 0))
    count = len(sources)
    return pl.pallas_call(
        functools.partial(turn_kernel, None, turned, scales),
        grid=(rows // step,),
        in_specs=[table, table] + [block] * count + [single] * count,
        out_specs=[block] * count,
        out_shape=[jax.ShapeDtypeStruct((rows, width), BF16)] * count,
        cost_estimate=pl.CostEstimate(
            flops=10 * rows * width * count, bytes_accessed=6 * rows * width * count, transcendentals=0
        ),
    )(*tables, *sources, *biases)


def wide_tables(position):
    lane = jnp.arange(PAIR, dtype=jnp.int32) % HD
    halves = ROT // 2
    rates = jnp.power(10000.0, -2.0 * jnp.arange(halves, dtype=F32) / ROT)[lane % halves]
    angles = position.astype(F32)[:, None] * rates[None, :]
    cosine = jnp.where(lane < ROT, jnp.cos(angles), 1.0)
    sine = jnp.sin(angles)
    signed = jnp.where(lane < halves, -sine, jnp.where(lane < ROT, sine, 0.0))
    return cosine, signed


def settle(value):
    return lax.optimization_barrier(value.astype(BF16))


def pair_sum(value):
    own = settle(value)
    other = lax.ppermute(own, "tp", [(0, 1), (1, 0)])
    return own.astype(F32) + other.astype(F32)


def ctx_sum(value):
    ctx, rank = lax.axis_size("ctx"), lax.axis_index("ctx")
    bits = [1 << b for b in range(ctx.bit_length() - 1)]
    held = settle(value)
    for bit in bits:
        rows = held.shape[0] // 2
        upper = (rank // bit) % 2
        keep = lax.dynamic_slice_in_dim(held, upper * rows, rows, 0)
        give = lax.dynamic_slice_in_dim(held, (1 - upper) * rows, rows, 0)
        got = lax.ppermute(give, "ctx", [(s, s ^ bit) for s in range(ctx)])
        held = settle(keep.astype(F32) + got.astype(F32))
    for bit in bits[::-1]:
        upper = (rank // bit) % 2
        got = lax.ppermute(held, "ctx", [(s, s ^ bit) for s in range(ctx)])
        lower_part = jnp.where(upper == 0, held, got)
        upper_part = jnp.where(upper == 0, got, held)
        held = jnp.concatenate([lower_part, upper_part])
    return held.astype(F32)


def after(value, *earlier):
    return lax.optimization_barrier((value, *earlier))[0]


def on_device(
    tokens,
    lengths,
    cotangent,
    first_gain,
    first_bias,
    second_gain,
    second_bias,
    w_qkv,
    b_qkv,
    w_out,
    b_out,
    w_up,
    b_up,
    w_down,
    b_down,
):
    token_rows, model = tokens.shape
    ctx = lax.axis_size("ctx")
    row_total = token_rows * ctx
    rank = lax.axis_index("ctx")
    place_first = rank * token_rows
    longest = row_total // 2
    behind = min(-(-(longest - 1) // token_rows), ctx - 1)
    small = jnp.stack([first_gain, first_bias, second_gain, second_bias, b_out, b_down])
    small = lax.all_gather(small, "fsdp", axis=1, tiled=True).astype(F32)
    gain_one, bias_one, gain_two, bias_two, out_bias, down_bias = [small[i] for i in range(6)]
    qkv_full = lax.all_gather(w_qkv, "fsdp", axis=1, tiled=True)
    up_full = lax.all_gather(w_up, "fsdp", axis=0, tiled=True)
    down_full = lax.all_gather(w_down, "fsdp", axis=1, tiled=True)
    out_full = lax.all_gather(w_out, "fsdp", axis=1, tiled=True)

    seq_ends = jnp.cumsum(lengths[0])
    starts = seq_ends - lengths[0]
    places = place_first + jnp.arange(token_rows, dtype=jnp.int32)
    inside = (places[:, None] >= starts[None, :]) & (places[:, None] < seq_ends[None, :])
    start = jnp.sum(jnp.where(inside, starts[None, :], 0), axis=1).astype(jnp.int32)
    tables = wide_tables(places - start)
    shift = place_first - behind * token_rows
    start_ext = start - shift
    place_ext = places - shift
    rows = [jnp.broadcast_to(r[None, :], (8, token_rows)) for r in (start_ext, place_ext)]
    low = start_ext[::BQ] // BK
    full = -(-start_ext[BQ - 1 :: BQ] // BK)
    base = behind * token_rows
    near = [r - base for r in rows]
    near_bounds = (jnp.maximum(low - base // BK, 0), jnp.maximum(full - base // BK, 0))

    x = tokens.astype(F32)
    centre = x - jnp.mean(x, axis=-1, keepdims=True)
    scale = lax.rsqrt(jnp.mean(centre * centre, axis=-1, keepdims=True) + 1e-05)
    normal = centre * scale
    normed_one = (normal * gain_one + bias_one).astype(BF16)
    normed_two = (normal * gain_two + bias_two).astype(BF16)

    linear = [dot(normed_one, qkv_full[i]) for i in range(3)]
    lifted = [jnp.broadcast_to(b_qkv[i].astype(F32)[None, :], (8, b_qkv.shape[1])) for i in range(3)]
    queries, keys, values = turn(
        tables, linear, lifted, (True, True, False), (HD**-0.5, 1.0, 1.0)
    )
    far_keys, far_values = [], []
    for back in range(behind, 0, -1):
        ahead = [(s, s + back) for s in range(ctx - back)]
        far_keys.append(lax.ppermute(keys, "ctx", ahead))
        far_values.append(lax.ppermute(values, "ctx", ahead))
    keys_far, values_far = jnp.concatenate(far_keys), jnp.concatenate(far_values)
    keys_all, values_all = jnp.concatenate([keys_far, keys]), jnp.concatenate([values_far, values])

    hidden_pre = dot(normed_two, up_full) + b_up.astype(F32)
    hidden, gelu_pull = jax.vjp(lambda v: jax.nn.gelu(v, approximate=False), hidden_pre)
    hidden = hidden.astype(BF16)
    grad_attention = after(dot(cotangent, out_full, NT).astype(BF16), hidden_pre)
    attention, lse, delta = attention_call(
        forward_kernel, base, (low, full), queries, keys_all, values_all, grad_attention, rows, (), "forward"
    )
    dq_far, dk_far, dv_far = attention_call(
        backward_kernel, base, (low, full), queries, keys_far, values_far, grad_attention, rows, (lse, delta), BF16
    )
    arrived_keys, arrived_values = [], []
    for index, back in enumerate(range(behind, 0, -1)):
        returning = [(s + back, s) for s in range(ctx - back)]
        cut = slice(index * token_rows, (index + 1) * token_rows)
        arrived_keys.append(lax.ppermute(dk_far[cut], "ctx", returning))
        arrived_values.append(lax.ppermute(dv_far[cut], "ctx", returning))

    grad_hidden = dot(after(cotangent, dk_far), down_full, NT)
    grad_hidden_pre = gelu_pull(grad_hidden)[0].astype(BF16)
    grad_w_down = dot(hidden, cotangent, TN)
    grad_w_up = dot(normed_two, grad_hidden_pre, TN)
    grad_b_up = jnp.sum(grad_hidden_pre.astype(F32), axis=0)
    error_two = dot(grad_hidden_pre, up_full, NT)

    grad_w_down, grad_w_up = grad_w_down.astype(BF16), grad_w_up.astype(BF16)
    part_down = ctx_sum(lax.psum_scatter(grad_w_down, "fsdp", scatter_dimension=1, tiled=True))
    part_up = ctx_sum(lax.psum_scatter(grad_w_up, "fsdp", scatter_dimension=0, tiled=True))

    near_g = after(grad_attention, grad_w_down, grad_w_up)
    dq_near, dk_near, dv_near = attention_call(
        backward_kernel, 0, near_bounds, queries, keys, values, near_g, near, (lse, delta), F32
    )
    branches = pair_sum(dot(attention, out_full) + dot(hidden, down_full))
    block_output = (x + branches + out_bias + down_bias).astype(BF16)

    zero = jnp.zeros((8, queries.shape[1]), F32)
    undo = (tables[0], -tables[1])
    (grad_linear_q,) = turn(undo, [dq_far + dq_near], [zero], (True,), (1.0,))
    grad_k = functools.reduce(lambda a, b: a + b.astype(F32), arrived_keys, dk_near)
    grad_v = functools.reduce(lambda a, b: a + b.astype(F32), arrived_values, dv_near)
    grad_linear_k, grad_linear_v = turn(undo, [grad_k, grad_v], [zero, zero], (True, False), (1.0, 1.0))
    grad_linear = [grad_linear_q, grad_linear_k, grad_linear_v]
    joined = [dot(normed_one, part, TN).astype(BF16) for part in grad_linear]
    joined.append(dot(cotangent, attention, TN).astype(BF16))
    joined = jnp.concatenate(joined, axis=1)
    joined = lax.psum_scatter(joined, "fsdp", scatter_dimension=0, tiled=True)
    grad_b_qkv = [jnp.sum(part.astype(F32), axis=0) for part in grad_linear]
    error_one = sum(dot(part, qkv_full[i], NT) for i, part in enumerate(grad_linear))

    whole = pair_sum(error_one * gain_one + error_two * gain_two)
    grad_tokens = cotangent.astype(F32) + scale * (
        whole
        - jnp.mean(whole, axis=-1, keepdims=True)
        - normal * jnp.mean(whole * normal, axis=-1, keepdims=True)
    )
    shared = jnp.concatenate(
        [
            jnp.sum(error_one * normal, axis=0),
            jnp.sum(error_one, axis=0),
            jnp.sum(error_two * normal, axis=0),
            jnp.sum(error_two, axis=0),
        ]
    )
    shared = shared + lax.ppermute(shared, "tp", [(0, 1), (1, 0)])
    grad_bias = jnp.sum(cotangent.astype(F32), axis=0)
    vector = lax.psum(jnp.concatenate([shared, grad_bias, *grad_b_qkv, grad_b_up]), ("fsdp", "ctx"))
    joined = lax.psum(after(joined, vector), "ctx").astype(F32)
    width = b_qkv.shape[1]
    part_qkv = jnp.stack([joined[:, i * width : (i + 1) * width] for i in range(3)])
    part_out = joined[:, 3 * width :].T
    owned = first_gain.shape[0]
    mine = lax.dynamic_slice_in_dim(
        vector[: 5 * model].reshape(5, model), lax.axis_index("fsdp") * owned, owned, 1
    )
    rest = vector[5 * model :]
    return (
        block_output,
        grad_tokens,
        mine[0],
        mine[1],
        mine[2],
        mine[3],
        part_qkv,
        rest[: 3 * width].reshape(3, width),
        part_out,
        mine[4],
        part_up,
        rest[3 * width :],
        part_down,
        mine[4],
    )


def solution(mesh):
    placed = (
        P(("fsdp", "ctx"), None),
        P("fsdp", None),
        P(("fsdp", "ctx"), None),
        P("fsdp"),
        P("fsdp"),
        P("fsdp"),
        P("fsdp"),
        P(None, "fsdp", "tp"),
        P(None, "tp"),
        P("tp", "fsdp"),
        P("fsdp"),
        P("fsdp", "tp"),
        P("tp"),
        P("tp", "fsdp"),
        P("fsdp"),
    )
    return jax.shard_map(
        on_device,
        mesh=mesh,
        in_specs=placed,
        out_specs=(
            P(("fsdp", "ctx"), None),
            P(("fsdp", "ctx"), None),
            P("fsdp"),
            P("fsdp"),
            P("fsdp"),
            P("fsdp"),
            P(None, "fsdp", "tp"),
            P(None, "tp"),
            P("tp", "fsdp"),
            P("fsdp"),
            P("fsdp", "tp"),
            P("tp"),
            P("tp", "fsdp"),
            P("fsdp"),
        ),
        check_vma=False,
    )
```
